32 devices in a mesh: obs: 8 (over z, y), coef: 4 (over x, core).
Axes of the slice: x: 2, y: 2, z: 4, core: 2. Of those that a mesh axis runs over, the one named last changes fastest.
Arguments:
- design: bfloat16 [8192, 36864], P('obs', 'coef'), may hold values from -0.03125 to 0.03125
- observations: bfloat16 [8, 8192], P(None, 'obs'), may hold values from -6 to 6
- shift_table: float32 [16], replicated, may hold values from 0.1 to 3
- shift_index: int32 [8], replicated, may hold values from 0 to 15
- coef_perm: int32 [36864], P('coef'), may hold values from 0 to 36863, as said below
- order_map: int32 [8], replicated, may hold values from 0 to 7, each once
Outputs:
- band_fourier: float32 [192, 2, 8, 32], P('coef', None, None, 'obs')
- field: float32 [8, 32, 1024], P(None, ('obs', 'coef'))
The draws below stay inside these ranges and needn't reach their ends.
Inputs may be any that keep to these rules, and one draw needn't show every extreme that they name: coef_perm is a permutation; the design columns of each block of 9216 consecutive columns hold exactly 1152 values of each range of 4608 consecutive values. `order_map`: each block number appears once.
All inputs are finite; a program needn't handle non-finite values.
Results may differ from the reference program's by a relative error of at most 0.007.
Values may be sent and summed in bfloat16 or wider, within the bound.
A program may use at most 64 MiB of HBM per device.

```python
import math
import jax
import jax.numpy as jnp
from jax import lax

NL = 192
COLS = 8
ITERS = 2
NSHIFT = 16
NLON = 1024
K = 36864
M = 8192
KDEV = 9216
NBLK = 8
OB = 24
KB = 1152
NLAT = 32
N_COEF = 4


def shuffle_block(block_key):
    return jax.random.permutation(block_key, OB * NL).astype(jnp.int32)


def shuffle_columns(column_key):
    return jax.random.permutation(column_key, KDEV).astype(jnp.int32)


def draw_coef_perm(key, part):
    block_size = OB * NL
    block_keys = jax.random.split(jax.random.fold_in(key, 11), NBLK)
    inside = jax.vmap(shuffle_block)(block_keys)
    values = inside + (jnp.arange(NBLK, dtype=jnp.int32) * block_size)[:, None]
    values = values.reshape(NBLK, N_COEF, KB).transpose(1, 0, 2).reshape(N_COEF, KDEV)
    column_keys = jax.random.split(jax.random.fold_in(key, 23), N_COEF)
    orders = jax.vmap(shuffle_columns)(column_keys)
    shuffled = jnp.take_along_axis(values, orders, axis=1)
    return shuffled.reshape(K).astype(jnp.int32)


def touch_ends(values, own_key, least, largest):
    longest = values.shape.index(max(values.shape))
    spots = []
    for shift in (0, 1):
        where = [jax.random.randint(jax.random.fold_in(own_key, axis), (), 0, length) for axis, length in enumerate(values.shape)]
        where[longest] = (where[longest] + shift) % values.shape[longest]
        spots.append(tuple(where))
    return values.at[spots[0]].set(least).at[spots[1]].set(largest)


def steps_of(key, shape, cuts, smallest, high):
    def one(axis_at, blocks):
        heights = jax.random.uniform(jax.random.fold_in(jax.random.fold_in(key, 6), axis_at), (blocks,), jnp.float32, smallest / len(cuts), high / len(cuts))
        return jnp.repeat(jnp.exp(heights), shape[axis_at] // blocks).reshape((-1,) + (1,) * (len(shape) - axis_at - 1))

    gain = one(*cuts[0])
    for cut in cuts[1:]:
        gain = gain * one(*cut)
    return gain


def normal_values(key, shape, spread, bound, cuts=(), kind=jnp.bfloat16):
    entries = spread * jax.random.normal(key, shape, jnp.float32)
    if cuts:
        entries = entries * steps_of(key, shape, cuts, -0.22, 0.18)
    return jnp.clip(entries, -bound, bound).astype(kind)


def setup_inputs(seed: int = 0) -> dict:
    key_list = jax.random.split(jax.random.key(seed), 7)
    design = normal_values(key_list[0], (M, K), K ** -0.5, 0.03125, ((0, 8), (1, 4)))
    observations = normal_values(key_list[1], (COLS, M), 1.0, 6.0, ((1, 8),))
    shift_table = jnp.clip(jnp.exp(jax.random.uniform(key_list[2], (NSHIFT,), jnp.float32, math.log(0.1), math.log(3.0))), 0.1, 3.0)
    shift_index = touch_ends(jax.random.randint(key_list[3], (COLS,), 0, NSHIFT), jax.random.fold_in(key_list[3], 1), 0, NSHIFT - 1).astype(jnp.int32)
    coef_perm = draw_coef_perm(jax.random.fold_in(key_list[6], 71), 0)
    order_map = jax.random.permutation(key_list[5], NBLK).astype(jnp.int32)
    return {"design": design, "observations": observations, "shift_table": shift_table, "shift_index": shift_index, "coef_perm": coef_perm, "order_map": order_map}


CENTRE_OFFSET = 1.25
HALF_WIDTH = 0.95

def legendre_table(orders, colatitude, degrees):
    cosine = jnp.cos(colatitude)
    sine = jnp.sin(colatitude)
    order_value = orders.astype(sine.dtype)[:, None]

    def advance(carry, degree):
        diagonal, previous, earlier = carry
        level = degree.astype(sine.dtype)
        safe_level = jnp.maximum(level, 1.0)
        grown = diagonal * sine * jnp.sqrt((2.0 * safe_level + 1.0) / (2.0 * safe_level))
        diagonal_next = jnp.where(degree == 0, jnp.ones_like(sine), jnp.where(degree == 1, jnp.sqrt(3.0) * sine, grown))
        above = level > order_value
        product = (level - order_value) * (level + order_value)
        denom = jnp.where(above, product, 1.0)
        first = jnp.sqrt(jnp.maximum((2.0 * level - 1.0) * (2.0 * level + 1.0), 0.0) / denom)
        second = jnp.sqrt(jnp.maximum((2.0 * level + 1.0) * (level + order_value - 1.0) * (level - order_value - 1.0), 0.0) / (denom * jnp.maximum(2.0 * level - 3.0, 1.0)))
        recur = first * cosine[None, :] * previous - second * earlier
        value = jnp.where(above, recur, jnp.where(level == order_value, diagonal_next[None, :], 0.0))
        return ((diagonal_next, value, previous), value)
    start = jnp.zeros((orders.shape[0], colatitude.shape[0]), sine.dtype)
    final_state, table = lax.scan(advance, (jnp.zeros_like(sine), start, start), jnp.arange(degrees, dtype=jnp.int32))
    return table

def wave_tables(rows, longitudes):
    steps_k = jnp.arange(longitudes, dtype=jnp.int32)
    scale = 2.0 * math.pi / longitudes
    cos_angle = (rows[:, None] * steps_k[None, :] % longitudes).astype(jnp.float32) * scale
    sin_angle = ((NL - rows)[:, None] * steps_k[None, :] % longitudes).astype(jnp.float32) * scale
    return (jnp.cos(cos_angle), jnp.sin(sin_angle))

def reference(design, observations, shift_table, shift_index, coef_perm, order_map):
    table_index = jnp.arange(NSHIFT, dtype=jnp.int32)
    shifts = lax.optimization_barrier(jnp.sum(jnp.where(shift_index[:, None] == table_index[None, :], shift_table[None, :], 0.0), axis=1))
    centre = shifts + CENTRE_OFFSET
    ratio_start = centre / HALF_WIDTH
    residual = jnp.dot(observations, design, preferred_element_type=jnp.float32)
    solution = jnp.zeros_like(residual)
    factor = 1.0 / ratio_start
    direction = residual / centre[:, None]
    for iteration in range(ITERS):
        solution = solution + direction
        image = lax.dot_general(direction.astype(jnp.bfloat16), design, (((1,), (1,)), ((), ())), preferred_element_type=jnp.float32)
        normal = jnp.dot(image.astype(jnp.bfloat16), design, preferred_element_type=jnp.float32)
        residual = residual - (normal + shifts[:, None] * direction)
        factor_next = 1.0 / (2.0 * ratio_start - factor)
        direction = (factor_next * factor)[:, None] * direction + (2.0 * factor_next / HALF_WIDTH)[:, None] * residual
        factor = factor_next
    solution = solution + direction
    paired = jnp.zeros((COLS, K), jnp.float32).at[:, coef_perm].set(solution).reshape(COLS, NL, NL)
    rows_all = jnp.arange(NL, dtype=jnp.int32)
    colatitude = math.pi * (jnp.arange(NLAT, dtype=jnp.int32).astype(jnp.float32) + 0.5) / NLAT
    cos_leg = legendre_table(rows_all, colatitude, NL)
    sin_leg = legendre_table(NL - rows_all, colatitude, NL)
    roll_index = (rows_all[None, :] - rows_all[:, None]) % NL
    shifted = jnp.take_along_axis(paired, roll_index[None, :, :], axis=2)
    cos_part = jnp.einsum('dqt,cqd->qct', cos_leg, shifted, precision=lax.Precision.HIGHEST)
    sin_part = jnp.einsum('dqt,cqd->qct', sin_leg, paired, precision=lax.Precision.HIGHEST)
    fourier = jnp.stack([cos_part, sin_part], axis=1) / math.sqrt(NL)
    owner_rows = (order_map[:, None] * OB + jnp.arange(OB, dtype=jnp.int32)[None, :]).reshape(NL)
    band_fourier = fourier[owner_rows]
    wave_cos, wave_sin = wave_tables(rows_all, NLON)
    dims = (((0,), (0,)), ((), ()))
    field = (lax.dot_general(fourier[:, 0].reshape(NL, COLS * NLAT), wave_cos, dims, precision=lax.Precision.HIGHEST) + lax.dot_general(fourier[:, 1].reshape(NL, COLS * NLAT), wave_sin, dims, precision=lax.Precision.HIGHEST)) / math.sqrt(NL)
    return (band_fourier, field.reshape(COLS, NLAT, NLON))
```

```python
import functools
import math

import jax
import jax.numpy as jnp
from jax import lax
from jax.experimental import pallas as pl
from jax.experimental.pallas import tpu as pltpu
from jax.sharding import PartitionSpec as P

NL = 192
COLS = 8
ITERS = 2
NSHIFT = 16
BPO = 2
NLON = 1024
LAT_DEV = 1

CENTRE_OFFSET = 1.25
HALF_WIDTH = 0.95
VMEM_SPEC = pl.BlockSpec(memory_space=pltpu.VMEM)
MESH = pl.DeviceIdType.MESH


def greet(axis, n, me):
    barrier = pltpu.get_barrier_semaphore()
    for step in range(1, n):
        pl.semaphore_signal(
            barrier, inc=1, device_id={axis: lax.rem(me + step, n)}, device_id_type=MESH
        )
    pl.semaphore_wait(barrier, n - 1)


def push(axis, n, me, step, src, dst, send_sem, recv_sem):
    return pltpu.make_async_remote_copy(
        src_ref=src,
        dst_ref=dst,
        send_sem=send_sem.at[step],
        recv_sem=recv_sem.at[step],
        device_id={axis: lax.rem(me + step, n)},
        device_id_type=MESH,
    )


def normal_kernel(
    n, mode, part_ref, res_ref, dir_ref, sol_ref, shift_ref, keep_ref, gain_ref,
    res_out, dir_out, sol_out, full_out,
    landed, gathered, send_a, recv_a, send_b, recv_b,
):
    me = lax.axis_index("obs")
    chunk = res_ref.shape[1]
    greet("obs", n, me)
    copies = []
    for step in range(1, n):
        target = lax.rem(me + step, n)
        src = part_ref.at[:, pl.ds(pl.multiple_of(target * chunk, 128), chunk)]
        copy = push("obs", n, me, step, src, landed.at[step], send_a, recv_a)
        copy.start()
        copies.append(copy)
    total = part_ref[:, pl.ds(pl.multiple_of(me * chunk, 128), chunk)]
    for step in range(1, n):
        copies[step - 1].wait()
        total = total + landed[step]
    if mode == 0:
        residual = total
        direction = residual / keep_ref[...]
        solution = direction
    else:
        direction = dir_ref[...]
        residual = res_ref[...] - (total + shift_ref[...] * direction)
        direction = keep_ref[...] * direction + gain_ref[...] * residual
        solution = sol_ref[...] + direction
    res_out[...] = residual
    dir_out[...] = direction
    sol_out[...] = solution
    sent = solution if mode == 2 else direction
    gathered[0] = sent.astype(jnp.bfloat16)
    copies = []
    for step in range(1, n):
        copy = push("obs", n, me, step, gathered.at[0], gathered.at[step], send_b, recv_b)
        copy.start()
        copies.append(copy)
    for step in range(n):
        if step:
            copies[step - 1].wait()
        origin = lax.rem(me + n - step, n)
        full_out[:, pl.ds(pl.multiple_of(origin * chunk, 128), chunk)] = gathered[step]


def normal_exchange(mode, n, partial, residual, direction, solution, shift, keep, gain):
    chunk = residual.shape[1]
    shard = jax.ShapeDtypeStruct((COLS, chunk), jnp.float32)
    return pl.pallas_call(
        functools.partial(normal_kernel, n, mode),
        out_shape=(shard, shard, shard, jax.ShapeDtypeStruct(partial.shape, jnp.bfloat16)),
        in_specs=[VMEM_SPEC] * 7,
        out_specs=(VMEM_SPEC,) * 4,
        scratch_shapes=[
            pltpu.VMEM((n, COLS, chunk), jnp.float32),
            pltpu.VMEM((n, COLS, chunk), jnp.bfloat16),
        ]
        + [pltpu.SemaphoreType.DMA((n,))] * 4,
        compiler_params=pltpu.CompilerParams(collective_id=mode, has_side_effects=True),
        name="normal_exchange",
    )(partial, residual, direction, solution, shift, keep, gain)


def sum_kernel(n, x_ref, o_ref, landed, send_sem, recv_sem):
    me = lax.axis_index("coef")
    greet("coef", n, me)
    copies = []
    for step in range(1, n):
        copy = push("coef", n, me, step, x_ref, landed.at[step], send_sem, recv_sem)
        copy.start()
        copies.append(copy)
    total = x_ref[...]
    for step in range(1, n):
        copies[step - 1].wait()
        total = total + landed[step]
    o_ref[...] = total.astype(o_ref.dtype)


def coef_sum(partial, n, cid):
    return pl.pallas_call(
        functools.partial(sum_kernel, n),
        out_shape=jax.ShapeDtypeStruct(partial.shape, jnp.bfloat16),
        in_specs=[VMEM_SPEC],
        out_specs=VMEM_SPEC,
        scratch_shapes=[pltpu.VMEM((n,) + partial.shape, jnp.float32)]
        + [pltpu.SemaphoreType.DMA((n,))] * 2,
        compiler_params=pltpu.CompilerParams(collective_id=cid, has_side_effects=True),
        name="coef_sum",
    )(partial)


def scatter_kernel(n, x_ref, o_ref, landed, send_sem, recv_sem):
    me = lax.axis_index("coef")
    greet("coef", n, me)
    copies = []
    for step in range(1, n):
        target = lax.rem(me + step, n)
        copy = push("coef", n, me, step, x_ref.at[target], landed.at[step], send_sem, recv_sem)
        copy.start()
        copies.append(copy)
    total = x_ref[me].astype(jnp.float32)
    for step in range(1, n):
        copies[step - 1].wait()
        total = total + landed[step].astype(jnp.float32)
    o_ref[...] = total


def coef_scatter(parts, n, cid):
    return pl.pallas_call(
        functools.partial(scatter_kernel, n),
        out_shape=jax.ShapeDtypeStruct(parts.shape[1:], jnp.float32),
        in_specs=[VMEM_SPEC],
        out_specs=VMEM_SPEC,
        scratch_shapes=[pltpu.VMEM(parts.shape, parts.dtype)]
        + [pltpu.SemaphoreType.DMA((n,))] * 2,
        compiler_params=pltpu.CompilerParams(collective_id=cid, has_side_effects=True),
        name="coef_scatter",
    )(parts)


def place_kernel(width, row_ref, col_ref, sol_ref, out_ref, spread):
    out_ref[...] = jnp.zeros_like(out_ref)
    wide = jnp.zeros((COLS, width), jnp.int32)

    def step(index, carry):
        at = pl.ds(pl.multiple_of(index * width, 128), width)
        values = sol_ref[:, at].astype(jnp.float32)
        rows = row_ref[:, at] + wide
        for pair in range(NL // 2):
            first = jnp.where(rows == 2 * pair, values, 0.0)
            second = jnp.where(rows == 2 * pair + 1, values, 0.0)
            both = jnp.concatenate([first, second], axis=0)
            spread[pair * 2 * COLS : (pair + 1) * 2 * COLS, :] = both.astype(jnp.bfloat16)
        degree = lax.broadcasted_iota(jnp.int32, (NL, width), 0)
        hot = jnp.where(degree == col_ref[:, at], 1.0, 0.0).astype(jnp.bfloat16)
        out_ref[...] += lax.dot_general(
            spread[...], hot, (((1,), (1,)), ((), ())), preferred_element_type=jnp.float32
        )
        return carry

    lax.fori_loop(0, sol_ref.shape[1] // width, step, 0)


def place(rows, cols, sol):
    kdev = sol.shape[1]
    width = next(w for w in (512, 384, 256, 128) if kdev % w == 0)
    return pl.pallas_call(
        functools.partial(place_kernel, width),
        out_shape=jax.ShapeDtypeStruct((NL * COLS, NL), jnp.float32),
        in_specs=[VMEM_SPEC] * 3,
        out_specs=VMEM_SPEC,
        scratch_shapes=[pltpu.VMEM((NL * COLS, width), jnp.bfloat16)],
        compiler_params=pltpu.CompilerParams(vmem_limit_bytes=32 << 20),
        name="place",
    )(rows, cols, sol)


def table_of(level, order, valid):
    product = (level - order) * (level + order)
    denom = jnp.where(valid, product, 1.0)
    first = jnp.sqrt(jnp.maximum((2.0 * level - 1.0) * (2.0 * level + 1.0), 0.0) / denom)
    second = jnp.sqrt(
        jnp.maximum((2.0 * level + 1.0) * (level + order - 1.0) * (level - order - 1.0), 0.0)
        / (denom * jnp.maximum(2.0 * level - 3.0, 1.0))
    )
    return jnp.where(valid, first, 0.0), jnp.where(valid, second, 0.0)


def legendre_kernel(order_ref, cos_ref, sin_ref, w_ref, out_ref, a_c, b_c, a_s, b_s, grow):
    lats, lanes = cos_ref.shape
    order = order_ref[0:1, :]
    other = float(NL) - order
    count = lax.broadcasted_iota(jnp.int32, (NL, lanes), 0).astype(jnp.float32)
    wide = jnp.zeros((NL, lanes), jnp.float32)
    low = order + wide
    high = other + wide
    level = count + low
    a, b = table_of(level, low, jnp.logical_and(count > 0.0, level < float(NL)))
    a_c[...] = a
    b_c[...] = b
    a, b = table_of(count, high, count > high)
    a_s[...] = a
    b_s[...] = b
    safe = jnp.maximum(count, 1.0)
    grow[...] = jnp.where(
        count == 1.0, math.sqrt(3.0), jnp.sqrt((2.0 * safe + 1.0) / (2.0 * safe))
    )
    cosine = cos_ref[...]
    sine = sin_ref[...]
    zero = cosine * 0.0
    low = order_ref[...]
    high = float(NL) - low

    def climb(degree, carry):
        diag, dc, ds = carry
        diag = diag * sine * grow[pl.ds(degree, 1), :]
        here = degree.astype(jnp.float32)
        return diag, jnp.where(low == here, diag, dc), jnp.where(high == here, diag, ds)

    start = zero + 1.0
    _, dc, ds = lax.fori_loop(
        1, NL, climb, (start, jnp.where(low == 0.0, start, zero), zero), unroll=4
    )
    acc_c = dc * w_ref[pl.ds(0, 1), :]

    def advance(column, carry):
        pc, ec, ps, es, acc_c, acc_s = carry
        at = pl.ds(column, 1)
        w = w_ref[at, :]
        vc = a_c[at, :] * cosine * pc - b_c[at, :] * ec
        begin = jnp.where(high == column.astype(jnp.float32), ds, 0.0)
        vs = a_s[at, :] * cosine * ps - b_s[at, :] * es + begin
        return vc, pc, vs, ps, acc_c + vc * w, acc_s + vs * w

    _, _, _, _, acc_c, acc_s = lax.fori_loop(
        1, NL, advance, (dc, zero, zero, zero, acc_c, zero), unroll=4
    )
    out_ref[0] = acc_c / math.sqrt(NL)
    out_ref[1] = acc_s / math.sqrt(NL)


def legendre(orders, colatitude, w):
    lanes = w.shape[1]
    lats = colatitude.shape[0]
    spread = jnp.zeros((lats, lanes), jnp.float32)
    table = pltpu.VMEM((NL, lanes), jnp.float32)
    return pl.pallas_call(
        legendre_kernel,
        out_shape=jax.ShapeDtypeStruct((2, lats, lanes), jnp.float32),
        in_specs=[VMEM_SPEC] * 4,
        out_specs=VMEM_SPEC,
        scratch_shapes=[table] * 5,
        name="legendre",
    )(
        orders[None, :] + spread,
        jnp.cos(colatitude)[:, None] + spread,
        jnp.sin(colatitude)[:, None] + spread,
        w,
    )


def wave_tables(rows, longitudes):
    steps_k = jnp.arange(longitudes, dtype=jnp.int32)
    scale = 2.0 * math.pi / longitudes
    cos_angle = (rows[:, None] * steps_k[None, :] % longitudes).astype(jnp.float32) * scale
    sin_angle = ((NL - rows)[:, None] * steps_k[None, :] % longitudes).astype(jnp.float32) * scale
    return (jnp.cos(cos_angle), jnp.sin(sin_angle))


def body(design, observations, shift_table, shift_index, coef_perm, order_map):
    obs_count = lax.axis_size("obs")
    coef_count = lax.axis_size("coef")
    coef_rank = lax.axis_index("coef")
    obs_rank = lax.axis_index("obs")
    kdev = design.shape[1]
    chunk = kdev // obs_count
    direct = chunk % 128 == 0
    table_index = jnp.arange(NSHIFT, dtype=jnp.int32)
    shifts = jnp.sum(
        jnp.where(shift_index[:, None] == table_index[None, :], shift_table[None, :], 0.0), axis=1
    )
    centre = shifts + CENTRE_OFFSET
    ratio_start = centre / HALF_WIDTH

    if direct:
        residual = direction = solution = jnp.zeros((COLS, chunk), jnp.float32)

    def exchange(mode, partial, state, keep, gain):
        residual, direction, solution = state
        if direct:
            residual, direction, solution, full = normal_exchange(
                mode, obs_count, partial, residual, direction, solution,
                shifts[:, None], keep[:, None], gain[:, None],
            )
            return (residual, direction, solution), full
        total = lax.psum(partial, "obs")
        if mode == 0:
            residual = total
            direction = residual / keep[:, None]
            solution = direction
        else:
            residual = residual - (total + shifts[:, None] * direction)
            direction = keep[:, None] * direction + gain[:, None] * residual
            solution = solution + direction
        full = solution if mode == 2 else direction
        return (residual, direction, solution), full.astype(jnp.bfloat16)

    empty = jnp.zeros((COLS, chunk if direct else kdev), jnp.float32)
    rhs = jnp.dot(observations, design, preferred_element_type=jnp.float32)
    state, full = exchange(0, rhs, (empty, empty, empty), centre, centre)
    factor = 1.0 / ratio_start
    for iteration in range(ITERS):
        partial_image = lax.dot_general(
            full, design, (((1,), (1,)), ((), ())), preferred_element_type=jnp.float32
        )
        image = coef_sum(partial_image, coef_count, 3 + iteration)
        partial = jnp.dot(image, design, preferred_element_type=jnp.float32)
        factor_next = 1.0 / (2.0 * ratio_start - factor)
        last = iteration == ITERS - 1
        state, full = exchange(
            2 if last else 1, partial, state, factor_next * factor, 2.0 * factor_next / HALF_WIDTH
        )
        factor = factor_next
    block_count = coef_count * BPO
    block_rows = NL // block_count
    owned_rows = kdev // NL
    block_ids = jnp.arange(block_count, dtype=jnp.int32)
    position = jnp.sum(
        jnp.where(order_map[:, None] == block_ids[None, :], block_ids[:, None], 0), axis=0
    )
    paired_row = coef_perm // NL
    column = coef_perm % NL
    place_of = jnp.sum(
        jnp.where(
            (paired_row // block_rows)[None, :] == block_ids[:, None], position[:, None], 0
        ),
        axis=0,
    )
    owner_row = place_of * block_rows + paired_row % block_rows
    placed = place(owner_row[None, :], column[None, :], full)
    lanes = owned_rows * COLS
    outgoing = placed.astype(jnp.bfloat16).reshape(coef_count, lanes, NL)
    local = coef_scatter(outgoing, coef_count, 5).T
    my_blocks = lax.dynamic_slice_in_dim(order_map, coef_rank * BPO, BPO)
    row_offsets = jnp.arange(block_rows, dtype=jnp.int32)
    owned_canon = (my_blocks[:, None] * block_rows + row_offsets[None, :]).reshape(owned_rows)
    lat_block = LAT_DEV * coef_count
    lat_total = lat_block * obs_count
    lat_ids = obs_rank * lat_block + jnp.arange(lat_block, dtype=jnp.int32)
    colatitude = math.pi * (lat_ids.astype(jnp.float32) + 0.5) / lat_total
    orders = jnp.repeat(owned_canon, COLS).astype(jnp.float32)
    parts = legendre(orders, colatitude, local).reshape(2, lat_block, owned_rows, COLS)
    band = parts.transpose(2, 0, 3, 1)
    own_cos, own_sin = wave_tables(owned_canon, NLON)
    first_sum = jnp.einsum("lqc,qk->lck", parts[0], own_cos, precision=lax.Precision.HIGHEST)
    second_sum = jnp.einsum("lqc,qk->lck", parts[1], own_sin, precision=lax.Precision.HIGHEST)
    shares = ((first_sum + second_sum) / math.sqrt(NL)).reshape(
        coef_count, LAT_DEV * COLS, NLON
    )
    field = coef_scatter(shares, coef_count, 6).reshape(LAT_DEV, COLS, NLON).transpose(1, 0, 2)
    return (band, field)


def solution(mesh):
    placed = (P("obs", "coef"), P(None, "obs"), P(), P(), P("coef"), P())
    return jax.shard_map(
        body,
        mesh=mesh,
        in_specs=placed,
        out_specs=(P("coef", None, None, "obs"), P(None, ("obs", "coef"), None)),
        check_vma=False,
    )
```

```python
import functools
import math

import jax
import jax.numpy as jnp
from jax import lax
from jax.experimental import pallas as pl
from jax.experimental.pallas import tpu as pltpu
from jax.sharding import PartitionSpec as P

NL = 192
COLS = 8
ITERS = 2
NSHIFT = 16
BPO = 2
NLON = 1024
LAT_DEV = 1

CENTRE_OFFSET = 1.25
HALF_WIDTH = 0.95
VMEM_SPEC = pl.BlockSpec(memory_space=pltpu.VMEM)
MESH = pl.DeviceIdType.MESH


def greet(axis, n, me):
    barrier = pltpu.get_barrier_semaphore()
    for step in range(1, n):
        pl.semaphore_signal(
            barrier, inc=1, device_id={axis: lax.rem(me + step, n)}, device_id_type=MESH
        )
    pl.semaphore_wait(barrier, n - 1)


def push(axis, n, me, step, src, dst, send_sem, recv_sem):
    return pltpu.make_async_remote_copy(
        src_ref=src,
        dst_ref=dst,
        send_sem=send_sem.at[step],
        recv_sem=recv_sem.at[step],
        device_id={axis: lax.rem(me + step, n)},
        device_id_type=MESH,
    )


def solver_kernel(
    n, nc, obs_ref, design_ref, shift_ref, keep_ref, gain_ref, full_out,
    held, part, landed, gathered, image_sent, image_landed,
    load_sem, send_a, recv_a, send_b, recv_b, send_c, recv_c,
):
    me = lax.axis_index("obs")
    mine = lax.axis_index("coef")
    chunk = part.shape[2]

    def load(step):
        block = lax.rem(me + step, n)
        return pltpu.make_async_copy(
            design_ref.at[:, pl.ds(pl.multiple_of(block * chunk, 128), chunk)],
            held.at[step],
            load_sem.at[step],
        )

    for step in list(range(1, n)) + [0]:
        load(step).start()
    barrier = pltpu.get_barrier_semaphore()
    for axis, count, rank in (("obs", n, me), ("coef", nc, mine)):
        for step in range(1, count):
            pl.semaphore_signal(
                barrier,
                inc=1,
                device_id={axis: lax.rem(rank + step, count)},
                device_id_type=MESH,
            )
    pl.semaphore_wait(barrier, n + nc - 2)

    def scatter_copy(rnd, step):
        return push(
            "obs", n, me, step, part.at[step], landed.at[rnd, step], send_a.at[rnd], recv_a.at[rnd]
        )

    def gather_copy(rnd, step):
        return push(
            "obs", n, me, step, gathered.at[rnd, 0], gathered.at[rnd, step],
            send_b.at[rnd], recv_b.at[rnd],
        )

    def image_copy(rnd, step):
        return push(
            "coef", nc, mine, step, image_sent, image_landed.at[rnd, step],
            send_c.at[rnd], recv_c.at[rnd],
        )

    def transposed_pass(rnd, left):
        def compute(step, carry):
            if rnd == 0:
                load(step).wait()
            part[step] = jnp.dot(left, held[step], preferred_element_type=jnp.float32)
            scatter_copy(rnd, step).start()
            return carry

        lax.fori_loop(1, n, compute, 0)
        if rnd == 0:
            load(0).wait()
        total = jnp.dot(left, held[0], preferred_element_type=jnp.float32)
        for step in range(1, n):
            scatter_copy(rnd, step).wait()
            total = total + landed[rnd, step]
        return total

    def gather(rnd, value):
        gathered[rnd, 0] = value.astype(jnp.bfloat16)
        for step in range(1, n):
            gather_copy(rnd, step).start()

    def image_of(rnd):
        image_sent[...] = jnp.zeros_like(image_sent)

        def compute(step, carry):
            @pl.when(step > 0)
            def _():
                gather_copy(rnd, step).wait()

            image_sent[...] += lax.dot_general(
                gathered[rnd, step],
                held[lax.rem(n - step, n)],
                (((1,), (1,)), ((), ())),
                preferred_element_type=jnp.float32,
            )
            return carry

        lax.fori_loop(0, n, compute, 0)
        for step in range(1, nc):
            image_copy(rnd, step).start()
        image = image_sent[...]
        for step in range(1, nc):
            image_copy(rnd, step).wait()
            image = image + image_landed[rnd, step]
        return image.astype(jnp.bfloat16)

    residual = transposed_pass(0, obs_ref[...])
    direction = residual / keep_ref[0]
    solution = direction
    gather(0, direction)
    for rnd in range(1, ITERS + 1):
        total = transposed_pass(rnd, image_of(rnd - 1))
        residual = residual - (total + shift_ref[...] * direction)
        direction = keep_ref[rnd] * direction + gain_ref[rnd] * residual
        solution = solution + direction
        gather(rnd, solution if rnd == ITERS else direction)
    for step in range(n):
        if step:
            gather_copy(ITERS, step).wait()
        origin = lax.rem(me + n - step, n)
        full_out[:, pl.ds(pl.multiple_of(origin * chunk, 128), chunk)] = gathered[ITERS, step]


def solve(n, nc, observations, design, shift, keep, gain):
    rows, kdev = design.shape
    chunk = kdev // n
    rounds = ITERS + 1
    return pl.pallas_call(
        functools.partial(solver_kernel, n, nc),
        out_shape=jax.ShapeDtypeStruct((COLS, kdev), jnp.bfloat16),
        in_specs=[VMEM_SPEC, pl.BlockSpec(memory_space=pl.ANY)] + [VMEM_SPEC] * 3,
        out_specs=VMEM_SPEC,
        scratch_shapes=[
            pltpu.VMEM((n, rows, chunk), jnp.bfloat16),
            pltpu.VMEM((n, COLS, chunk), jnp.float32),
            pltpu.VMEM((rounds, n, COLS, chunk), jnp.float32),
            pltpu.VMEM((rounds, n, COLS, chunk), jnp.bfloat16),
            pltpu.VMEM((COLS, rows), jnp.float32),
            pltpu.VMEM((ITERS, nc, COLS, rows), jnp.float32),
            pltpu.SemaphoreType.DMA((n,)),
        ]
        + [pltpu.SemaphoreType.DMA((rounds, n))] * 4
        + [pltpu.SemaphoreType.DMA((ITERS, nc))] * 2,
        compiler_params=pltpu.CompilerParams(
            collective_id=0, has_side_effects=True, vmem_limit_bytes=48 << 20
        ),
        name="solve",
    )(observations, design, shift, keep, gain)


def sum_kernel(n, x_ref, o_ref, landed, send_sem, recv_sem):
    me = lax.axis_index("coef")
    greet("coef", n, me)
    copies = []
    for step in range(1, n):
        copy = push("coef", n, me, step, x_ref, landed.at[step], send_sem, recv_sem)
        copy.start()
        copies.append(copy)
    total = x_ref[...]
    for step in range(1, n):
        copies[step - 1].wait()
        total = total + landed[step]
    o_ref[...] = total.astype(o_ref.dtype)


def coef_sum(partial, n, cid):
    return pl.pallas_call(
        functools.partial(sum_kernel, n),
        out_shape=jax.ShapeDtypeStruct(partial.shape, jnp.bfloat16),
        in_specs=[VMEM_SPEC],
        out_specs=VMEM_SPEC,
        scratch_shapes=[pltpu.VMEM((n,) + partial.shape, jnp.float32)]
        + [pltpu.SemaphoreType.DMA((n,))] * 2,
        compiler_params=pltpu.CompilerParams(collective_id=cid, has_side_effects=True),
        name="coef_sum",
    )(partial)


def solve_plain(nc, observations, design, shift, keep, gain):
    def transposed_pass(left):
        return lax.psum(jnp.dot(left, design, preferred_element_type=jnp.float32), "obs")

    residual = transposed_pass(observations)
    direction = residual / keep[0]
    solution = direction
    for rnd in range(1, ITERS + 1):
        partial_image = lax.dot_general(
            direction.astype(jnp.bfloat16),
            design,
            (((1,), (1,)), ((), ())),
            preferred_element_type=jnp.float32,
        )
        total = transposed_pass(coef_sum(partial_image, nc, 2 + rnd))
        residual = residual - (total + shift * direction)
        direction = keep[rnd] * direction + gain[rnd] * residual
        solution = solution + direction
    return solution.astype(jnp.bfloat16)


def scatter_kernel(n, x_ref, o_ref, landed, send_sem, recv_sem):
    me = lax.axis_index("coef")
    greet("coef", n, me)
    copies = []
    for step in range(1, n):
        target = lax.rem(me + step, n)
        copy = push("coef", n, me, step, x_ref.at[target], landed.at[step], send_sem, recv_sem)
        copy.start()
        copies.append(copy)
    total = x_ref[me].astype(jnp.float32)
    for step in range(1, n):
        copies[step - 1].wait()
        total = total + landed[step].astype(jnp.float32)
    o_ref[...] = total


def coef_scatter(parts, n, cid):
    return pl.pallas_call(
        functools.partial(scatter_kernel, n),
        out_shape=jax.ShapeDtypeStruct(parts.shape[1:], jnp.float32),
        in_specs=[VMEM_SPEC],
        out_specs=VMEM_SPEC,
        scratch_shapes=[pltpu.VMEM(parts.shape, parts.dtype)]
        + [pltpu.SemaphoreType.DMA((n,))] * 2,
        compiler_params=pltpu.CompilerParams(collective_id=cid, has_side_effects=True),
        name="coef_scatter",
    )(parts)


def place_kernel(width, row_ref, col_ref, sol_ref, out_ref, spread):
    out_ref[...] = jnp.zeros_like(out_ref)
    wide = jnp.zeros((COLS, width), jnp.int32)

    def step(index, carry):
        at = pl.ds(pl.multiple_of(index * width, 128), width)
        values = sol_ref[:, at].astype(jnp.float32)
        rows = row_ref[:, at] + wide
        for pair in range(NL // 2):
            first = jnp.where(rows == 2 * pair, values, 0.0)
            second = jnp.where(rows == 2 * pair + 1, values, 0.0)
            both = jnp.concatenate([first, second], axis=0)
            spread[pair * 2 * COLS : (pair + 1) * 2 * COLS, :] = both.astype(jnp.bfloat16)
        degree = lax.broadcasted_iota(jnp.int32, (NL, width), 0)
        hot = jnp.where(degree == col_ref[:, at], 1.0, 0.0).astype(jnp.bfloat16)
        out_ref[...] += lax.dot_general(
            spread[...], hot, (((1,), (1,)), ((), ())), preferred_element_type=jnp.float32
        )
        return carry

    lax.fori_loop(0, sol_ref.shape[1] // width, step, 0)


def place(rows, cols, sol):
    kdev = sol.shape[1]
    width = next(w for w in (512, 384, 256, 128) if kdev % w == 0)
    return pl.pallas_call(
        functools.partial(place_kernel, width),
        out_shape=jax.ShapeDtypeStruct((NL * COLS, NL), jnp.float32),
        in_specs=[VMEM_SPEC] * 3,
        out_specs=VMEM_SPEC,
        scratch_shapes=[pltpu.VMEM((NL * COLS, width), jnp.bfloat16)],
        compiler_params=pltpu.CompilerParams(vmem_limit_bytes=32 << 20),
        name="place",
    )(rows, cols, sol)


def table_of(level, order, valid):
    product = (level - order) * (level + order)
    denom = jnp.where(valid, product, 1.0)
    first = jnp.sqrt(jnp.maximum((2.0 * level - 1.0) * (2.0 * level + 1.0), 0.0) / denom)
    second = jnp.sqrt(
        jnp.maximum((2.0 * level + 1.0) * (level + order - 1.0) * (level - order - 1.0), 0.0)
        / (denom * jnp.maximum(2.0 * level - 3.0, 1.0))
    )
    return jnp.where(valid, first, 0.0), jnp.where(valid, second, 0.0)


def legendre_kernel(order_ref, cos_ref, sin_ref, w_ref, out_ref, a_c, b_c, a_s, b_s, grow):
    lats, lanes = cos_ref.shape
    order = order_ref[0:1, :]
    other = float(NL) - order
    count = lax.broadcasted_iota(jnp.int32, (NL, lanes), 0).astype(jnp.float32)
    wide = jnp.zeros((NL, lanes), jnp.float32)
    low = order + wide
    high = other + wide
    level = count + low
    a, b = table_of(level, low, jnp.logical_and(count > 0.0, level < float(NL)))
    a_c[...] = a
    b_c[...] = b
    a, b = table_of(count, high, count > high)
    a_s[...] = a
    b_s[...] = b
    safe = jnp.maximum(count, 1.0)
    grow[...] = jnp.where(
        count == 1.0, math.sqrt(3.0), jnp.sqrt((2.0 * safe + 1.0) / (2.0 * safe))
    )
    cosine = cos_ref[...]
    sine = sin_ref[...]
    zero = cosine * 0.0
    low = order_ref[...]
    high = float(NL) - low

    def climb(degree, carry):
        diag, dc, ds = carry
        diag = diag * sine * grow[pl.ds(degree, 1), :]
        here = degree.astype(jnp.float32)
        return diag, jnp.where(low == here, diag, dc), jnp.where(high == here, diag, ds)

    start = zero + 1.0
    _, dc, ds = lax.fori_loop(
        1, NL, climb, (start, jnp.where(low == 0.0, start, zero), zero), unroll=4
    )
    acc_c = dc * w_ref[pl.ds(0, 1), :]

    def advance(column, carry):
        pc, ec, ps, es, acc_c, acc_s = carry
        at = pl.ds(column, 1)
        w = w_ref[at, :]
        vc = a_c[at, :] * cosine * pc - b_c[at, :] * ec
        begin = jnp.where(high == column.astype(jnp.float32), ds, 0.0)
        vs = a_s[at, :] * cosine * ps - b_s[at, :] * es + begin
        return vc, pc, vs, ps, acc_c + vc * w, acc_s + vs * w

    _, _, _, _, acc_c, acc_s = lax.fori_loop(
        1, NL, advance, (dc, zero, zero, zero, acc_c, zero), unroll=4
    )
    out_ref[0] = acc_c / math.sqrt(NL)
    out_ref[1] = acc_s / math.sqrt(NL)


def legendre(orders, colatitude, w):
    lanes = w.shape[1]
    lats = colatitude.shape[0]
    spread = jnp.zeros((lats, lanes), jnp.float32)
    table = pltpu.VMEM((NL, lanes), jnp.float32)
    return pl.pallas_call(
        legendre_kernel,
        out_shape=jax.ShapeDtypeStruct((2, lats, lanes), jnp.float32),
        in_specs=[VMEM_SPEC] * 4,
        out_specs=VMEM_SPEC,
        scratch_shapes=[table] * 5,
        name="legendre",
    )(
        orders[None, :] + spread,
        jnp.cos(colatitude)[:, None] + spread,
        jnp.sin(colatitude)[:, None] + spread,
        w,
    )


def wave_tables(rows, longitudes):
    steps_k = jnp.arange(longitudes, dtype=jnp.int32)
    scale = 2.0 * math.pi / longitudes
    cos_angle = (rows[:, None] * steps_k[None, :] % longitudes).astype(jnp.float32) * scale
    sin_angle = ((NL - rows)[:, None] * steps_k[None, :] % longitudes).astype(jnp.float32) * scale
    return (jnp.cos(cos_angle), jnp.sin(sin_angle))


def body(design, observations, shift_table, shift_index, coef_perm, order_map):
    obs_count = lax.axis_size("obs")
    coef_count = lax.axis_size("coef")
    coef_rank = lax.axis_index("coef")
    obs_rank = lax.axis_index("obs")
    kdev = design.shape[1]
    chunk = kdev // obs_count
    direct = chunk % 128 == 0
    table_index = jnp.arange(NSHIFT, dtype=jnp.int32)
    shifts = jnp.sum(
        jnp.where(shift_index[:, None] == table_index[None, :], shift_table[None, :], 0.0), axis=1
    )
    centre = shifts + CENTRE_OFFSET
    ratio_start = centre / HALF_WIDTH

    keep = [centre]
    gain = [centre]
    factor = 1.0 / ratio_start
    for iteration in range(ITERS):
        factor_next = 1.0 / (2.0 * ratio_start - factor)
        keep.append(factor_next * factor)
        gain.append(2.0 * factor_next / HALF_WIDTH)
        factor = factor_next
    keep = jnp.stack(keep)[:, :, None]
    gain = jnp.stack(gain)[:, :, None]
    if direct:
        full = solve(
            obs_count, coef_count, observations, design, shifts[:, None], keep, gain
        )
    else:
        full = solve_plain(coef_count, observations, design, shifts[:, None], keep, gain)
    block_count = coef_count * BPO
    block_rows = NL // block_count
    owned_rows = kdev // NL
    block_ids = jnp.arange(block_count, dtype=jnp.int32)
    position = jnp.sum(
        jnp.where(order_map[:, None] == block_ids[None, :], block_ids[:, None], 0), axis=0
    )
    paired_row = coef_perm // NL
    column = coef_perm % NL
    place_of = jnp.sum(
        jnp.where(
            (paired_row // block_rows)[None, :] == block_ids[:, None], position[:, None], 0
        ),
        axis=0,
    )
    owner_row = place_of * block_rows + paired_row % block_rows
    placed = place(owner_row[None, :], column[None, :], full)
    lanes = owned_rows * COLS
    outgoing = placed.astype(jnp.bfloat16).reshape(coef_count, lanes, NL)
    local = coef_scatter(outgoing, coef_count, 5).T
    my_blocks = lax.dynamic_slice_in_dim(order_map, coef_rank * BPO, BPO)
    row_offsets = jnp.arange(block_rows, dtype=jnp.int32)
    owned_canon = (my_blocks[:, None] * block_rows + row_offsets[None, :]).reshape(owned_rows)
    lat_block = LAT_DEV * coef_count
    lat_total = lat_block * obs_count
    lat_ids = obs_rank * lat_block + jnp.arange(lat_block, dtype=jnp.int32)
    colatitude = math.pi * (lat_ids.astype(jnp.float32) + 0.5) / lat_total
    orders = jnp.repeat(owned_canon, COLS).astype(jnp.float32)
    parts = legendre(orders, colatitude, local).reshape(2, lat_block, owned_rows, COLS)
    band = parts.transpose(2, 0, 3, 1)
    own_cos, own_sin = wave_tables(owned_canon, NLON)
    first_sum = jnp.einsum("lqc,qk->lck", parts[0], own_cos, precision=lax.Precision.HIGHEST)
    second_sum = jnp.einsum("lqc,qk->lck", parts[1], own_sin, precision=lax.Precision.HIGHEST)
    shares = ((first_sum + second_sum) / math.sqrt(NL)).reshape(
        coef_count, LAT_DEV * COLS, NLON
    )
    field = coef_scatter(shares, coef_count, 6).reshape(LAT_DEV, COLS, NLON).transpose(1, 0, 2)
    return (band, field)


def solution(mesh):
    placed = (P("obs", "coef"), P(None, "obs"), P(), P(), P("coef"), P())
    return jax.shard_map(
        body,
        mesh=mesh,
        in_specs=placed,
        out_specs=(P("coef", None, None, "obs"), P(None, ("obs", "coef"), None)),
        check_vma=False,
    )
```

```python
import functools
import math

import jax
import jax.numpy as jnp
from jax import lax
from jax.experimental import pallas as pl
from jax.experimental.pallas import tpu as pltpu
from jax.sharding import PartitionSpec as P

NL = 192
COLS = 8
ITERS = 2
NSHIFT = 16
BPO = 2
NLON = 1024
LAT_DEV = 1

CENTRE_OFFSET = 1.25
HALF_WIDTH = 0.95
VMEM_SPEC = pl.BlockSpec(memory_space=pltpu.VMEM)
MESH = pl.DeviceIdType.MESH


def greet(axis, n, me):
    barrier = pltpu.get_barrier_semaphore()
    for step in range(1, n):
        pl.semaphore_signal(
            barrier, inc=1, device_id={axis: lax.rem(me + step, n)}, device_id_type=MESH
        )
    pl.semaphore_wait(barrier, n - 1)


def push(axis, n, me, step, src, dst, send_sem, recv_sem):
    return pltpu.make_async_remote_copy(
        src_ref=src,
        dst_ref=dst,
        send_sem=send_sem.at[step],
        recv_sem=recv_sem.at[step],
        device_id={axis: lax.rem(me + step, n)},
        device_id_type=MESH,
    )


def solver_kernel(
    n, nc, obs_ref, design_ref, shift_ref, keep_ref, gain_ref, full_out,
    held, part, landed, gathered, image_sent, image_landed,
    load_sem, send_a, recv_a, send_b, recv_b, send_c, recv_c,
):
    me = lax.axis_index("obs")
    mine = lax.axis_index("coef")
    chunk = part.shape[2]

    def load(step):
        block = lax.rem(me + step, n)
        return pltpu.make_async_copy(
            design_ref.at[:, pl.ds(pl.multiple_of(block * chunk, 128), chunk)],
            held.at[step],
            load_sem.at[step],
        )

    for step in list(range(1, n)) + [0]:
        load(step).start()
    barrier = pltpu.get_barrier_semaphore()
    for axis, count, rank in (("obs", n, me), ("coef", nc, mine)):
        for step in range(1, count):
            pl.semaphore_signal(
                barrier,
                inc=1,
                device_id={axis: lax.rem(rank + step, count)},
                device_id_type=MESH,
            )
    pl.semaphore_wait(barrier, n + nc - 2)

    def scatter_copy(rnd, step):
        return push(
            "obs", n, me, step, part.at[step], landed.at[rnd, step], send_a.at[rnd], recv_a.at[rnd]
        )

    def gather_copy(rnd, step):
        return push(
            "obs", n, me, step, gathered.at[rnd, 0], gathered.at[rnd, step],
            send_b.at[rnd], recv_b.at[rnd],
        )

    def image_copy(rnd, step):
        return push(
            "coef", nc, mine, step, image_sent, image_landed.at[rnd, step],
            send_c.at[rnd], recv_c.at[rnd],
        )

    def transposed_pass(rnd, left):
        def compute(step, carry):
            if rnd == 0:
                load(step).wait()
            part[step] = jnp.dot(left, held[step], preferred_element_type=jnp.float32)
            scatter_copy(rnd, step).start()
            return carry

        lax.fori_loop(1, n, compute, 0)
        if rnd == 0:
            load(0).wait()
        total = jnp.dot(left, held[0], preferred_element_type=jnp.float32)
        for step in range(1, n):
            scatter_copy(rnd, step).wait()
            total = total + landed[rnd, step]
        return total

    def gather(rnd, value):
        gathered[rnd, 0] = value.astype(jnp.bfloat16)
        for step in range(1, n):
            gather_copy(rnd, step).start()

    def image_of(rnd):
        image_sent[...] = jnp.zeros_like(image_sent)

        def compute(step, carry):
            @pl.when(step > 0)
            def _():
                gather_copy(rnd, step).wait()

            image_sent[...] += lax.dot_general(
                gathered[rnd, step],
                held[lax.rem(n - step, n)],
                (((1,), (1,)), ((), ())),
                preferred_element_type=jnp.float32,
            )
            return carry

        lax.fori_loop(0, n, compute, 0)
        for step in range(1, nc):
            image_copy(rnd, step).start()
        image = image_sent[...]
        for step in range(1, nc):
            image_copy(rnd, step).wait()
            image = image + image_landed[rnd, step]
        return image.astype(jnp.bfloat16)

    residual = transposed_pass(0, obs_ref[...])
    direction = residual / keep_ref[0]
    solution = direction
    gather(0, direction)
    for rnd in range(1, ITERS + 1):
        total = transposed_pass(rnd, image_of(rnd - 1))
        residual = residual - (total + shift_ref[...] * direction)
        direction = keep_ref[rnd] * direction + gain_ref[rnd] * residual
        solution = solution + direction
        gather(rnd, solution if rnd == ITERS else direction)
    for step in range(n):
        if step:
            gather_copy(ITERS, step).wait()
        origin = lax.rem(me + n - step, n)
        full_out[:, pl.ds(pl.multiple_of(origin * chunk, 128), chunk)] = gathered[ITERS, step]


def solve(n, nc, observations, design, shift, keep, gain):
    rows, kdev = design.shape
    chunk = kdev // n
    rounds = ITERS + 1
    return pl.pallas_call(
        functools.partial(solver_kernel, n, nc),
        out_shape=jax.ShapeDtypeStruct((COLS, kdev), jnp.bfloat16),
        in_specs=[VMEM_SPEC, pl.BlockSpec(memory_space=pl.ANY)] + [VMEM_SPEC] * 3,
        out_specs=VMEM_SPEC,
        scratch_shapes=[
            pltpu.VMEM((n, rows, chunk), jnp.bfloat16),
            pltpu.VMEM((n, COLS, chunk), jnp.float32),
            pltpu.VMEM((rounds, n, COLS, chunk), jnp.float32),
            pltpu.VMEM((rounds, n, COLS, chunk), jnp.bfloat16),
            pltpu.VMEM((COLS, rows), jnp.float32),
            pltpu.VMEM((ITERS, nc, COLS, rows), jnp.float32),
            pltpu.SemaphoreType.DMA((n,)),
        ]
        + [pltpu.SemaphoreType.DMA((rounds, n))] * 4
        + [pltpu.SemaphoreType.DMA((ITERS, nc))] * 2,
        compiler_params=pltpu.CompilerParams(
            collective_id=0, has_side_effects=True, vmem_limit_bytes=48 << 20
        ),
        name="solve",
    )(observations, design, shift, keep, gain)


def sum_kernel(n, x_ref, o_ref, landed, send_sem, recv_sem):
    me = lax.axis_index("coef")
    greet("coef", n, me)
    copies = []
    for step in range(1, n):
        copy = push("coef", n, me, step, x_ref, landed.at[step], send_sem, recv_sem)
        copy.start()
        copies.append(copy)
    total = x_ref[...]
    for step in range(1, n):
        copies[step - 1].wait()
        total = total + landed[step]
    o_ref[...] = total.astype(o_ref.dtype)


def coef_sum(partial, n, cid):
    return pl.pallas_call(
        functools.partial(sum_kernel, n),
        out_shape=jax.ShapeDtypeStruct(partial.shape, jnp.bfloat16),
        in_specs=[VMEM_SPEC],
        out_specs=VMEM_SPEC,
        scratch_shapes=[pltpu.VMEM((n,) + partial.shape, jnp.float32)]
        + [pltpu.SemaphoreType.DMA((n,))] * 2,
        compiler_params=pltpu.CompilerParams(collective_id=cid, has_side_effects=True),
        name="coef_sum",
    )(partial)


def solve_plain(nc, observations, design, shift, keep, gain):
    def transposed_pass(left):
        return lax.psum(jnp.dot(left, design, preferred_element_type=jnp.float32), "obs")

    residual = transposed_pass(observations)
    direction = residual / keep[0]
    solution = direction
    for rnd in range(1, ITERS + 1):
        partial_image = lax.dot_general(
            direction.astype(jnp.bfloat16),
            design,
            (((1,), (1,)), ((), ())),
            preferred_element_type=jnp.float32,
        )
        total = transposed_pass(coef_sum(partial_image, nc, 2 + rnd))
        residual = residual - (total + shift * direction)
        direction = keep[rnd] * direction + gain[rnd] * residual
        solution = solution + direction
    return solution.astype(jnp.bfloat16)


def scatter_kernel(n, x_ref, o_ref, landed, send_sem, recv_sem):
    me = lax.axis_index("coef")
    greet("coef", n, me)
    copies = []
    for step in range(1, n):
        target = lax.rem(me + step, n)
        copy = push("coef", n, me, step, x_ref.at[target], landed.at[step], send_sem, recv_sem)
        copy.start()
        copies.append(copy)
    total = x_ref[me].astype(jnp.float32)
    for step in range(1, n):
        copies[step - 1].wait()
        total = total + landed[step].astype(jnp.float32)
    o_ref[...] = total


def coef_scatter(parts, n, cid):
    return pl.pallas_call(
        functools.partial(scatter_kernel, n),
        out_shape=jax.ShapeDtypeStruct(parts.shape[1:], jnp.float32),
        in_specs=[VMEM_SPEC],
        out_specs=VMEM_SPEC,
        scratch_shapes=[pltpu.VMEM(parts.shape, parts.dtype)]
        + [pltpu.SemaphoreType.DMA((n,))] * 2,
        compiler_params=pltpu.CompilerParams(collective_id=cid, has_side_effects=True),
        name="coef_scatter",
    )(parts)


def place_kernel(width, row_ref, col_ref, sol_ref, out_ref, spread):
    out_ref[...] = jnp.zeros_like(out_ref)
    wide = jnp.zeros((COLS, width), jnp.int32)

    def step(index, carry):
        at = pl.ds(pl.multiple_of(index * width, 128), width)
        values = sol_ref[:, at].astype(jnp.float32)
        rows = row_ref[:, at] + wide
        for pair in range(NL // 2):
            first = jnp.where(rows == 2 * pair, values, 0.0)
            second = jnp.where(rows == 2 * pair + 1, values, 0.0)
            both = jnp.concatenate([first, second], axis=0)
            spread[pair * 2 * COLS : (pair + 1) * 2 * COLS, :] = both.astype(jnp.bfloat16)
        degree = lax.broadcasted_iota(jnp.int32, (NL, width), 0)
        hot = jnp.where(degree == col_ref[:, at], 1.0, 0.0).astype(jnp.bfloat16)
        out_ref[...] += lax.dot_general(
            spread[...], hot, (((1,), (1,)), ((), ())), preferred_element_type=jnp.float32
        )
        return carry

    lax.fori_loop(0, sol_ref.shape[1] // width, step, 0)


def place(rows, cols, sol):
    kdev = sol.shape[1]
    width = next(w for w in (512, 384, 256, 128) if kdev % w == 0)
    return pl.pallas_call(
        functools.partial(place_kernel, width),
        out_shape=jax.ShapeDtypeStruct((NL * COLS, NL), jnp.float32),
        in_specs=[VMEM_SPEC] * 3,
        out_specs=VMEM_SPEC,
        scratch_shapes=[pltpu.VMEM((NL * COLS, width), jnp.bfloat16)],
        compiler_params=pltpu.CompilerParams(vmem_limit_bytes=32 << 20),
        name="place",
    )(rows, cols, sol)


def share_kernel(
    n, nc, width, row_ref, col_ref, sol_ref, out_ref,
    spread, acc, sent, landed, gathered, send_a, recv_a, send_b, recv_b,
):
    me = lax.axis_index("obs")
    mine = lax.axis_index("coef")
    owned = NL // nc
    sub = owned // n
    span = sub * COLS
    barrier = pltpu.get_barrier_semaphore()
    for axis, count, rank in (("obs", n, me), ("coef", nc, mine)):
        for step in range(1, count):
            pl.semaphore_signal(
                barrier,
                inc=1,
                device_id={axis: lax.rem(rank + step, count)},
                device_id_type=MESH,
            )
    acc[...] = jnp.zeros_like(acc)
    wide = jnp.zeros((COLS, width), jnp.int32)

    def step_of(index, carry):
        at = pl.ds(pl.multiple_of(index * width, 128), width)
        values = sol_ref[:, at].astype(jnp.float32)
        rows = row_ref[:, at] + wide - me * sub
        for pair in range(nc * sub // 2):
            halves = []
            for entry in (2 * pair, 2 * pair + 1):
                row = entry // sub * owned + entry % sub
                halves.append(jnp.where(rows == row, values, 0.0))
            both = jnp.concatenate(halves, axis=0)
            spread[pair * 2 * COLS : (pair + 1) * 2 * COLS, :] = both.astype(jnp.bfloat16)
        degree = lax.broadcasted_iota(jnp.int32, (NL, width), 0)
        hot = jnp.where(degree == col_ref[:, at], 1.0, 0.0).astype(jnp.bfloat16)
        acc[...] += lax.dot_general(
            spread[...], hot, (((1,), (1,)), ((), ())), preferred_element_type=jnp.float32
        )
        return carry

    lax.fori_loop(0, sol_ref.shape[1] // width, step_of, 0)
    for owner in range(nc):
        sent[owner] = acc[owner * span : (owner + 1) * span, :].astype(jnp.bfloat16)
    pl.semaphore_wait(barrier, n + nc - 2)
    copies = []
    for step in range(1, nc):
        target = lax.rem(mine + step, nc)
        copy = push("coef", nc, mine, step, sent.at[target], landed.at[step], send_a, recv_a)
        copy.start()
        copies.append(copy)
    total = sent[mine].astype(jnp.float32)
    for step in range(1, nc):
        copies[step - 1].wait()
        total = total + landed[step].astype(jnp.float32)
    gathered[0] = total.astype(jnp.bfloat16)
    copies = []
    for step in range(1, n):
        copy = push("obs", n, me, step, gathered.at[0], gathered.at[step], send_b, recv_b)
        copy.start()
        copies.append(copy)
    for step in range(n):
        if step:
            copies[step - 1].wait()
        origin = lax.rem(me + n - step, n)
        at = pl.ds(pl.multiple_of(origin * span, COLS), span)
        out_ref[at, :] = gathered[step].astype(jnp.float32)


def share(n, nc, rows, cols, sol):
    kdev = sol.shape[1]
    width = next(w for w in (1152, 512, 384, 256, 128) if kdev % w == 0)
    part = NL // n * COLS
    span = part // nc
    return pl.pallas_call(
        functools.partial(share_kernel, n, nc, width),
        out_shape=jax.ShapeDtypeStruct((n * span, NL), jnp.float32),
        in_specs=[VMEM_SPEC] * 3,
        out_specs=VMEM_SPEC,
        scratch_shapes=[
            pltpu.VMEM((part, width), jnp.bfloat16),
            pltpu.VMEM((part, NL), jnp.float32),
            pltpu.VMEM((nc, span, NL), jnp.bfloat16),
            pltpu.VMEM((nc, span, NL), jnp.bfloat16),
            pltpu.VMEM((n, span, NL), jnp.bfloat16),
        ]
        + [pltpu.SemaphoreType.DMA((nc,))] * 2
        + [pltpu.SemaphoreType.DMA((n,))] * 2,
        compiler_params=pltpu.CompilerParams(
            collective_id=1, has_side_effects=True, vmem_limit_bytes=32 << 20
        ),
        name="share",
    )(rows, cols, sol)


def table_of(level, order, valid):
    product = (level - order) * (level + order)
    denom = jnp.where(valid, product, 1.0)
    first = jnp.sqrt(jnp.maximum((2.0 * level - 1.0) * (2.0 * level + 1.0), 0.0) / denom)
    second = jnp.sqrt(
        jnp.maximum((2.0 * level + 1.0) * (level + order - 1.0) * (level - order - 1.0), 0.0)
        / (denom * jnp.maximum(2.0 * level - 3.0, 1.0))
    )
    return jnp.where(valid, first, 0.0), jnp.where(valid, second, 0.0)


def legendre_kernel(
    order_ref, cos_ref, sin_ref, local_ref, out_ref, a_c, b_c, a_s, b_s, grow, w_ref
):
    lats, lanes = cos_ref.shape
    w_ref[...] = local_ref[...].T
    order = order_ref[0:1, :]
    other = float(NL) - order
    count = lax.broadcasted_iota(jnp.int32, (NL, lanes), 0).astype(jnp.float32)
    wide = jnp.zeros((NL, lanes), jnp.float32)
    low = order + wide
    high = other + wide
    level = count + low
    a, b = table_of(level, low, jnp.logical_and(count > 0.0, level < float(NL)))
    a_c[...] = a
    b_c[...] = b
    a, b = table_of(count, high, count > high)
    a_s[...] = a
    b_s[...] = b
    safe = jnp.maximum(count, 1.0)
    grow[...] = jnp.where(
        count == 1.0, math.sqrt(3.0), jnp.sqrt((2.0 * safe + 1.0) / (2.0 * safe))
    )
    cosine = cos_ref[...]
    sine = sin_ref[...]
    zero = cosine * 0.0
    low = order_ref[...]
    high = float(NL) - low

    def climb(degree, carry):
        diag, dc, ds = carry
        diag = diag * sine * grow[pl.ds(degree, 1), :]
        here = degree.astype(jnp.float32)
        return diag, jnp.where(low == here, diag, dc), jnp.where(high == here, diag, ds)

    start = zero + 1.0
    _, dc, ds = lax.fori_loop(
        1, NL, climb, (start, jnp.where(low == 0.0, start, zero), zero), unroll=4
    )
    acc_c = dc * w_ref[pl.ds(0, 1), :]

    def advance(column, carry):
        pc, ec, ps, es, acc_c, acc_s = carry
        at = pl.ds(column, 1)
        w = w_ref[at, :]
        vc = a_c[at, :] * cosine * pc - b_c[at, :] * ec
        begin = jnp.where(high == column.astype(jnp.float32), ds, 0.0)
        vs = a_s[at, :] * cosine * ps - b_s[at, :] * es + begin
        return vc, pc, vs, ps, acc_c + vc * w, acc_s + vs * w

    _, _, _, _, acc_c, acc_s = lax.fori_loop(
        1, NL, advance, (dc, zero, zero, zero, acc_c, zero), unroll=4
    )
    out_ref[0] = acc_c / math.sqrt(NL)
    out_ref[1] = acc_s / math.sqrt(NL)


def legendre(orders, colatitude, w):
    lanes = w.shape[0]
    lats = colatitude.shape[0]
    spread = jnp.zeros((lats, lanes), jnp.float32)
    table = pltpu.VMEM((NL, lanes), jnp.float32)
    return pl.pallas_call(
        legendre_kernel,
        out_shape=jax.ShapeDtypeStruct((2, lats, lanes), jnp.float32),
        in_specs=[VMEM_SPEC] * 4,
        out_specs=VMEM_SPEC,
        scratch_shapes=[table] * 6,
        name="legendre",
    )(
        orders[None, :] + spread,
        jnp.cos(colatitude)[:, None] + spread,
        jnp.sin(colatitude)[:, None] + spread,
        w,
    )


def wave_tables(rows, longitudes):
    steps_k = jnp.arange(longitudes, dtype=jnp.int32)
    scale = 2.0 * math.pi / longitudes
    cos_angle = (rows[:, None] * steps_k[None, :] % longitudes).astype(jnp.float32) * scale
    sin_angle = ((NL - rows)[:, None] * steps_k[None, :] % longitudes).astype(jnp.float32) * scale
    return (jnp.cos(cos_angle), jnp.sin(sin_angle))


def body(design, observations, shift_table, shift_index, coef_perm, order_map):
    obs_count = lax.axis_size("obs")
    coef_count = lax.axis_size("coef")
    coef_rank = lax.axis_index("coef")
    obs_rank = lax.axis_index("obs")
    kdev = design.shape[1]
    chunk = kdev // obs_count
    direct = chunk % 128 == 0
    table_index = jnp.arange(NSHIFT, dtype=jnp.int32)
    shifts = jnp.sum(
        jnp.where(shift_index[:, None] == table_index[None, :], shift_table[None, :], 0.0), axis=1
    )
    centre = shifts + CENTRE_OFFSET
    ratio_start = centre / HALF_WIDTH

    keep = [centre]
    gain = [centre]
    factor = 1.0 / ratio_start
    for iteration in range(ITERS):
        factor_next = 1.0 / (2.0 * ratio_start - factor)
        keep.append(factor_next * factor)
        gain.append(2.0 * factor_next / HALF_WIDTH)
        factor = factor_next
    keep = jnp.stack(keep)[:, :, None]
    gain = jnp.stack(gain)[:, :, None]
    if direct:
        full = solve(
            obs_count, coef_count, observations, design, shifts[:, None], keep, gain
        )
    else:
        full = solve_plain(coef_count, observations, design, shifts[:, None], keep, gain)
    block_count = coef_count * BPO
    block_rows = NL // block_count
    owned_rows = kdev // NL
    block_ids = jnp.arange(block_count, dtype=jnp.int32)
    position = jnp.sum(
        jnp.where(order_map[:, None] == block_ids[None, :], block_ids[:, None], 0), axis=0
    )
    paired_row = coef_perm // NL
    column = coef_perm % NL
    place_of = jnp.sum(
        jnp.where(
            (paired_row // block_rows)[None, :] == block_ids[:, None], position[:, None], 0
        ),
        axis=0,
    )
    owner_row = place_of * block_rows + paired_row % block_rows
    lanes = owned_rows * COLS
    if direct and owned_rows % (2 * obs_count) == 0:
        local = share(obs_count, coef_count, owner_row[None, :], column[None, :], full)
    else:
        placed = place(owner_row[None, :], column[None, :], full)
        outgoing = placed.astype(jnp.bfloat16).reshape(coef_count, lanes, NL)
        local = coef_scatter(outgoing, coef_count, 5)
    my_blocks = lax.dynamic_slice_in_dim(order_map, coef_rank * BPO, BPO)
    row_offsets = jnp.arange(block_rows, dtype=jnp.int32)
    owned_canon = (my_blocks[:, None] * block_rows + row_offsets[None, :]).reshape(owned_rows)
    lat_block = LAT_DEV * coef_count
    lat_total = lat_block * obs_count
    lat_ids = obs_rank * lat_block + jnp.arange(lat_block, dtype=jnp.int32)
    colatitude = math.pi * (lat_ids.astype(jnp.float32) + 0.5) / lat_total
    orders = jnp.repeat(owned_canon, COLS).astype(jnp.float32)
    parts = legendre(orders, colatitude, local).reshape(2, lat_block, owned_rows, COLS)
    band = parts.transpose(2, 0, 3, 1)
    own_cos, own_sin = wave_tables(owned_canon, NLON)
    first_sum = jnp.einsum("lqc,qk->lck", parts[0], own_cos, precision=lax.Precision.HIGHEST)
    second_sum = jnp.einsum("lqc,qk->lck", parts[1], own_sin, precision=lax.Precision.HIGHEST)
    shares = ((first_sum + second_sum) / math.sqrt(NL)).reshape(
        coef_count, LAT_DEV * COLS, NLON
    )
    field = coef_scatter(shares, coef_count, 6).reshape(LAT_DEV, COLS, NLON).transpose(1, 0, 2)
    return (band, field)


def solution(mesh):
    placed = (P("obs", "coef"), P(None, "obs"), P(), P(), P("coef"), P())
    return jax.shard_map(
        body,
        mesh=mesh,
        in_specs=placed,
        out_specs=(P("coef", None, None, "obs"), P(None, ("obs", "coef"), None)),
        check_vma=False,
    )
```

```python
import functools
import math

import jax
import jax.numpy as jnp
from jax import lax
from jax.experimental import pallas as pl
from jax.experimental.pallas import tpu as pltpu
from jax.sharding import PartitionSpec as P

NL = 192
COLS = 8
ITERS = 2
NSHIFT = 16
BPO = 2
NLON = 1024
LAT_DEV = 1

CENTRE_OFFSET = 1.25
HALF_WIDTH = 0.95
VMEM_SPEC = pl.BlockSpec(memory_space=pltpu.VMEM)
MESH = pl.DeviceIdType.MESH


def greet(axis, n, me):
    barrier = pltpu.get_barrier_semaphore()
    for step in range(1, n):
        pl.semaphore_signal(
            barrier, inc=1, device_id={axis: lax.rem(me + step, n)}, device_id_type=MESH
        )
    pl.semaphore_wait(barrier, n - 1)


def push(axis, n, me, step, src, dst, send_sem, recv_sem):
    return pltpu.make_async_remote_copy(
        src_ref=src,
        dst_ref=dst,
        send_sem=send_sem.at[step],
        recv_sem=recv_sem.at[step],
        device_id={axis: lax.rem(me + step, n)},
        device_id_type=MESH,
    )


def solver_kernel(
    n, nc, obs_ref, design_ref, shift_ref, keep_ref, gain_ref, full_out,
    held, part, landed, gathered, image_sent, image_landed,
    load_sem, send_a, recv_a, send_b, recv_b, send_c, recv_c,
):
    me = lax.axis_index("obs")
    mine = lax.axis_index("coef")
    chunk = part.shape[2]

    def load(step):
        block = lax.rem(me + step, n)
        return pltpu.make_async_copy(
            design_ref.at[:, pl.ds(pl.multiple_of(block * chunk, 128), chunk)],
            held.at[step],
            load_sem.at[step],
        )

    for step in list(range(1, n)) + [0]:
        load(step).start()
    barrier = pltpu.get_barrier_semaphore()
    for axis, count, rank in (("obs", n, me), ("coef", nc, mine)):
        for step in range(1, count):
            pl.semaphore_signal(
                barrier,
                inc=1,
                device_id={axis: lax.rem(rank + step, count)},
                device_id_type=MESH,
            )
    pl.semaphore_wait(barrier, n + nc - 2)

    def scatter_copy(rnd, step):
        return push(
            "obs", n, me, step, part.at[step], landed.at[rnd, step], send_a.at[rnd], recv_a.at[rnd]
        )

    def gather_copy(rnd, step):
        return push(
            "obs", n, me, step, gathered.at[rnd, 0], gathered.at[rnd, step],
            send_b.at[rnd], recv_b.at[rnd],
        )

    def image_copy(rnd, step):
        return push(
            "coef", nc, mine, step, image_sent, image_landed.at[rnd, step],
            send_c.at[rnd], recv_c.at[rnd],
        )

    def transposed_pass(rnd, left):
        def compute(step, carry):
            if rnd == 0:
                load(step).wait()
            part[step] = jnp.dot(left, held[step], preferred_element_type=jnp.float32)
            scatter_copy(rnd, step).start()
            return carry

        lax.fori_loop(1, n, compute, 0, unroll=True)
        if rnd == 0:
            load(0).wait()
        total = jnp.dot(left, held[0], preferred_element_type=jnp.float32)
        for step in range(1, n):
            scatter_copy(rnd, step).wait()
            total = total + landed[rnd, step]
        return total

    def gather(rnd, value):
        gathered[rnd, 0] = value.astype(jnp.bfloat16)
        for step in range(1, n):
            gather_copy(rnd, step).start()

    def image_of(rnd):
        image_sent[...] = jnp.zeros_like(image_sent)

        def compute(step, carry):
            @pl.when(step > 0)
            def _():
                gather_copy(rnd, step).wait()

            image_sent[...] += lax.dot_general(
                gathered[rnd, step],
                held[lax.rem(n - step, n)],
                (((1,), (1,)), ((), ())),
                preferred_element_type=jnp.float32,
            )
            return carry

        lax.fori_loop(0, n, compute, 0, unroll=True)
        for step in range(1, nc):
            image_copy(rnd, step).start()
        image = image_sent[...]
        for step in range(1, nc):
            image_copy(rnd, step).wait()
            image = image + image_landed[rnd, step]
        return image.astype(jnp.bfloat16)

    residual = transposed_pass(0, obs_ref[...])
    direction = residual / keep_ref[0]
    solution = direction
    gather(0, direction)
    for rnd in range(1, ITERS + 1):
        total = transposed_pass(rnd, image_of(rnd - 1))
        residual = residual - (total + shift_ref[...] * direction)
        direction = keep_ref[rnd] * direction + gain_ref[rnd] * residual
        solution = solution + direction
        gather(rnd, solution if rnd == ITERS else direction)
    for step in range(n):
        if step:
            gather_copy(ITERS, step).wait()
        origin = lax.rem(me + n - step, n)
        full_out[:, pl.ds(pl.multiple_of(origin * chunk, 128), chunk)] = gathered[ITERS, step]


def solve(n, nc, observations, design, shift, keep, gain):
    rows, kdev = design.shape
    chunk = kdev // n
    rounds = ITERS + 1
    return pl.pallas_call(
        functools.partial(solver_kernel, n, nc),
        out_shape=jax.ShapeDtypeStruct((COLS, kdev), jnp.bfloat16),
        in_specs=[VMEM_SPEC, pl.BlockSpec(memory_space=pl.ANY)] + [VMEM_SPEC] * 3,
        out_specs=VMEM_SPEC,
        scratch_shapes=[
            pltpu.VMEM((n, rows, chunk), jnp.bfloat16),
            pltpu.VMEM((n, COLS, chunk), jnp.float32),
            pltpu.VMEM((rounds, n, COLS, chunk), jnp.float32),
            pltpu.VMEM((rounds, n, COLS, chunk), jnp.bfloat16),
            pltpu.VMEM((COLS, rows), jnp.float32),
            pltpu.VMEM((ITERS, nc, COLS, rows), jnp.float32),
            pltpu.SemaphoreType.DMA((n,)),
        ]
        + [pltpu.SemaphoreType.DMA((rounds, n))] * 4
        + [pltpu.SemaphoreType.DMA((ITERS, nc))] * 2,
        compiler_params=pltpu.CompilerParams(
            collective_id=0, has_side_effects=True, vmem_limit_bytes=48 << 20
        ),
        name="solve",
    )(observations, design, shift, keep, gain)


def sum_kernel(n, x_ref, o_ref, landed, send_sem, recv_sem):
    me = lax.axis_index("coef")
    greet("coef", n, me)
    copies = []
    for step in range(1, n):
        copy = push("coef", n, me, step, x_ref, landed.at[step], send_sem, recv_sem)
        copy.start()
        copies.append(copy)
    total = x_ref[...]
    for step in range(1, n):
        copies[step - 1].wait()
        total = total + landed[step]
    o_ref[...] = total.astype(o_ref.dtype)


def coef_sum(partial, n, cid):
    return pl.pallas_call(
        functools.partial(sum_kernel, n),
        out_shape=jax.ShapeDtypeStruct(partial.shape, jnp.bfloat16),
        in_specs=[VMEM_SPEC],
        out_specs=VMEM_SPEC,
        scratch_shapes=[pltpu.VMEM((n,) + partial.shape, jnp.float32)]
        + [pltpu.SemaphoreType.DMA((n,))] * 2,
        compiler_params=pltpu.CompilerParams(collective_id=cid, has_side_effects=True),
        name="coef_sum",
    )(partial)


def solve_plain(nc, observations, design, shift, keep, gain):
    def transposed_pass(left):
        return lax.psum(jnp.dot(left, design, preferred_element_type=jnp.float32), "obs")

    residual = transposed_pass(observations)
    direction = residual / keep[0]
    solution = direction
    for rnd in range(1, ITERS + 1):
        partial_image = lax.dot_general(
            direction.astype(jnp.bfloat16),
            design,
            (((1,), (1,)), ((), ())),
            preferred_element_type=jnp.float32,
        )
        total = transposed_pass(coef_sum(partial_image, nc, 2 + rnd))
        residual = residual - (total + shift * direction)
        direction = keep[rnd] * direction + gain[rnd] * residual
        solution = solution + direction
    return solution.astype(jnp.bfloat16)


def scatter_kernel(n, x_ref, o_ref, landed, send_sem, recv_sem):
    me = lax.axis_index("coef")
    greet("coef", n, me)
    copies = []
    for step in range(1, n):
        target = lax.rem(me + step, n)
        copy = push("coef", n, me, step, x_ref.at[target], landed.at[step], send_sem, recv_sem)
        copy.start()
        copies.append(copy)
    total = x_ref[me].astype(jnp.float32)
    for step in range(1, n):
        copies[step - 1].wait()
        total = total + landed[step].astype(jnp.float32)
    o_ref[...] = total


def coef_scatter(parts, n, cid):
    return pl.pallas_call(
        functools.partial(scatter_kernel, n),
        out_shape=jax.ShapeDtypeStruct(parts.shape[1:], jnp.float32),
        in_specs=[VMEM_SPEC],
        out_specs=VMEM_SPEC,
        scratch_shapes=[pltpu.VMEM(parts.shape, parts.dtype)]
        + [pltpu.SemaphoreType.DMA((n,))] * 2,
        compiler_params=pltpu.CompilerParams(collective_id=cid, has_side_effects=True),
        name="coef_scatter",
    )(parts)


def place_kernel(width, row_ref, col_ref, sol_ref, out_ref, spread):
    out_ref[...] = jnp.zeros_like(out_ref)
    wide = jnp.zeros((COLS, width), jnp.int32)

    def step(index, carry):
        at = pl.ds(pl.multiple_of(index * width, 128), width)
        values = sol_ref[:, at].astype(jnp.float32)
        rows = row_ref[:, at] + wide
        for pair in range(NL // 2):
            first = jnp.where(rows == 2 * pair, values, 0.0)
            second = jnp.where(rows == 2 * pair + 1, values, 0.0)
            both = jnp.concatenate([first, second], axis=0)
            spread[pair * 2 * COLS : (pair + 1) * 2 * COLS, :] = both.astype(jnp.bfloat16)
        degree = lax.broadcasted_iota(jnp.int32, (NL, width), 0)
        hot = jnp.where(degree == col_ref[:, at], 1.0, 0.0).astype(jnp.bfloat16)
        out_ref[...] += lax.dot_general(
            spread[...], hot, (((1,), (1,)), ((), ())), preferred_element_type=jnp.float32
        )
        return carry

    lax.fori_loop(0, sol_ref.shape[1] // width, step, 0)


def place(rows, cols, sol):
    kdev = sol.shape[1]
    width = next(w for w in (512, 384, 256, 128) if kdev % w == 0)
    return pl.pallas_call(
        functools.partial(place_kernel, width),
        out_shape=jax.ShapeDtypeStruct((NL * COLS, NL), jnp.float32),
        in_specs=[VMEM_SPEC] * 3,
        out_specs=VMEM_SPEC,
        scratch_shapes=[pltpu.VMEM((NL * COLS, width), jnp.bfloat16)],
        compiler_params=pltpu.CompilerParams(vmem_limit_bytes=32 << 20),
        name="place",
    )(rows, cols, sol)


def share_kernel(
    n, nc, width, row_ref, col_ref, sol_ref, out_ref,
    spread, acc, sent, landed, gathered, send_a, recv_a, send_b, recv_b,
):
    me = lax.axis_index("obs")
    mine = lax.axis_index("coef")
    owned = NL // nc
    sub = owned // n
    span = sub * COLS
    barrier = pltpu.get_barrier_semaphore()
    for axis, count, rank in (("obs", n, me), ("coef", nc, mine)):
        for step in range(1, count):
            pl.semaphore_signal(
                barrier,
                inc=1,
                device_id={axis: lax.rem(rank + step, count)},
                device_id_type=MESH,
            )
    acc[...] = jnp.zeros_like(acc)
    wide = jnp.zeros((COLS, width), jnp.int32)

    def step_of(index, carry):
        at = pl.ds(pl.multiple_of(index * width, 128), width)
        values = sol_ref[:, at].astype(jnp.float32)
        rows = row_ref[:, at] + wide - me * sub
        for pair in range(nc * sub // 2):
            halves = []
            for entry in (2 * pair, 2 * pair + 1):
                row = entry // sub * owned + entry % sub
                halves.append(jnp.where(rows == row, values, 0.0))
            both = jnp.concatenate(halves, axis=0)
            spread[pair * 2 * COLS : (pair + 1) * 2 * COLS, :] = both.astype(jnp.bfloat16)
        degree = lax.broadcasted_iota(jnp.int32, (NL, width), 0)
        hot = jnp.where(degree == col_ref[:, at], 1.0, 0.0).astype(jnp.bfloat16)
        acc[...] += lax.dot_general(
            spread[...], hot, (((1,), (1,)), ((), ())), preferred_element_type=jnp.float32
        )
        return carry

    lax.fori_loop(0, sol_ref.shape[1] // width, step_of, 0)
    for owner in range(nc):
        sent[owner] = acc[owner * span : (owner + 1) * span, :].astype(jnp.bfloat16)
    pl.semaphore_wait(barrier, n + nc - 2)
    copies = []
    for step in range(1, nc):
        target = lax.rem(mine + step, nc)
        copy = push("coef", nc, mine, step, sent.at[target], landed.at[step], send_a, recv_a)
        copy.start()
        copies.append(copy)
    total = sent[mine].astype(jnp.float32)
    for step in range(1, nc):
        copies[step - 1].wait()
        total = total + landed[step].astype(jnp.float32)
    gathered[0] = total.astype(jnp.bfloat16)
    copies = []
    for step in range(1, n):
        copy = push("obs", n, me, step, gathered.at[0], gathered.at[step], send_b, recv_b)
        copy.start()
        copies.append(copy)
    for step in range(n):
        if step:
            copies[step - 1].wait()
        origin = lax.rem(me + n - step, n)
        at = pl.ds(pl.multiple_of(origin * span, COLS), span)
        out_ref[at, :] = gathered[step].astype(jnp.float32)


def share(n, nc, rows, cols, sol):
    kdev = sol.shape[1]
    width = next(w for w in (1152, 512, 384, 256, 128) if kdev % w == 0)
    part = NL // n * COLS
    span = part // nc
    return pl.pallas_call(
        functools.partial(share_kernel, n, nc, width),
        out_shape=jax.ShapeDtypeStruct((n * span, NL), jnp.float32),
        in_specs=[VMEM_SPEC] * 3,
        out_specs=VMEM_SPEC,
        scratch_shapes=[
            pltpu.VMEM((part, width), jnp.bfloat16),
            pltpu.VMEM((part, NL), jnp.float32),
            pltpu.VMEM((nc, span, NL), jnp.bfloat16),
            pltpu.VMEM((nc, span, NL), jnp.bfloat16),
            pltpu.VMEM((n, span, NL), jnp.bfloat16),
        ]
        + [pltpu.SemaphoreType.DMA((nc,))] * 2
        + [pltpu.SemaphoreType.DMA((n,))] * 2,
        compiler_params=pltpu.CompilerParams(
            collective_id=1, has_side_effects=True, vmem_limit_bytes=32 << 20
        ),
        name="share",
    )(rows, cols, sol)


def table_of(level, order, valid):
    product = (level - order) * (level + order)
    denom = jnp.where(valid, product, 1.0)
    first = jnp.sqrt(jnp.maximum((2.0 * level - 1.0) * (2.0 * level + 1.0), 0.0) / denom)
    second = jnp.sqrt(
        jnp.maximum((2.0 * level + 1.0) * (level + order - 1.0) * (level - order - 1.0), 0.0)
        / (denom * jnp.maximum(2.0 * level - 3.0, 1.0))
    )
    return jnp.where(valid, first, 0.0), jnp.where(valid, second, 0.0)


def legendre_kernel(
    angle_ref, local_ref, out_ref, a_c, b_c, a_s, b_s, grow, w_ref
):
    lats, lanes = angle_ref.shape[1:]
    w_ref[...] = local_ref[...].T
    order = angle_ref[0, 0:1, :]
    other = float(NL) - order
    count = lax.broadcasted_iota(jnp.int32, (NL, lanes), 0).astype(jnp.float32)
    wide = jnp.zeros((NL, lanes), jnp.float32)
    low = order + wide
    high = other + wide
    level = count + low
    a, b = table_of(level, low, jnp.logical_and(count > 0.0, level < float(NL)))
    a_c[...] = a
    b_c[...] = b
    a, b = table_of(count, high, count > high)
    a_s[...] = a
    b_s[...] = b
    safe = jnp.maximum(count, 1.0)
    grow[...] = jnp.where(
        count == 1.0, math.sqrt(3.0), jnp.sqrt((2.0 * safe + 1.0) / (2.0 * safe))
    )
    cosine = angle_ref[1]
    sine = angle_ref[2]
    zero = cosine * 0.0
    low = angle_ref[0]
    high = float(NL) - low

    def climb(degree, carry):
        diag, dc, ds = carry
        diag = diag * sine * grow[pl.ds(degree, 1), :]
        here = degree.astype(jnp.float32)
        return diag, jnp.where(low == here, diag, dc), jnp.where(high == here, diag, ds)

    start = zero + 1.0
    _, dc, ds = lax.fori_loop(
        1, NL, climb, (start, jnp.where(low == 0.0, start, zero), zero), unroll=4
    )
    acc_c = dc * w_ref[pl.ds(0, 1), :]

    def advance(column, carry):
        pc, ec, ps, es, acc_c, acc_s = carry
        at = pl.ds(column, 1)
        w = w_ref[at, :]
        vc = a_c[at, :] * cosine * pc - b_c[at, :] * ec
        begin = jnp.where(high == column.astype(jnp.float32), ds, 0.0)
        vs = a_s[at, :] * cosine * ps - b_s[at, :] * es + begin
        return vc, pc, vs, ps, acc_c + vc * w, acc_s + vs * w

    _, _, _, _, acc_c, acc_s = lax.fori_loop(
        1, NL, advance, (dc, zero, zero, zero, acc_c, zero), unroll=4
    )
    out_ref[0] = acc_c / math.sqrt(NL)
    out_ref[1] = acc_s / math.sqrt(NL)


def legendre(orders, colatitude, w):
    lanes = w.shape[0]
    lats = colatitude.shape[0]
    which = lax.broadcasted_iota(jnp.int32, (3, lats, lanes), 0)
    angles = jnp.where(
        which == 0,
        orders[None, None, :],
        jnp.where(which == 1, jnp.cos(colatitude)[:, None], jnp.sin(colatitude)[:, None]),
    )
    table = pltpu.VMEM((NL, lanes), jnp.float32)
    return pl.pallas_call(
        legendre_kernel,
        out_shape=jax.ShapeDtypeStruct((2, lats, lanes), jnp.float32),
        in_specs=[VMEM_SPEC] * 2,
        out_specs=VMEM_SPEC,
        scratch_shapes=[table] * 6,
        name="legendre",
    )(
        angles,
        w,
    )


def wave_tables(rows, longitudes):
    steps_k = jnp.arange(longitudes, dtype=jnp.int32)
    scale = 2.0 * math.pi / longitudes
    cos_angle = (rows[:, None] * steps_k[None, :] % longitudes).astype(jnp.float32) * scale
    sin_angle = ((NL - rows)[:, None] * steps_k[None, :] % longitudes).astype(jnp.float32) * scale
    return (jnp.cos(cos_angle), jnp.sin(sin_angle))


def body(design, observations, shift_table, shift_index, coef_perm, order_map):
    obs_count = lax.axis_size("obs")
    coef_count = lax.axis_size("coef")
    coef_rank = lax.axis_index("coef")
    obs_rank = lax.axis_index("obs")
    kdev = design.shape[1]
    chunk = kdev // obs_count
    direct = chunk % 128 == 0
    table_index = jnp.arange(NSHIFT, dtype=jnp.int32)
    shifts = jnp.sum(
        jnp.where(shift_index[:, None] == table_index[None, :], shift_table[None, :], 0.0), axis=1
    )
    centre = shifts + CENTRE_OFFSET
    ratio_start = centre / HALF_WIDTH

    keep = [centre]
    gain = [centre]
    factor = 1.0 / ratio_start
    for iteration in range(ITERS):
        factor_next = 1.0 / (2.0 * ratio_start - factor)
        keep.append(factor_next * factor)
        gain.append(2.0 * factor_next / HALF_WIDTH)
        factor = factor_next
    keep = jnp.stack(keep)[:, :, None]
    gain = jnp.stack(gain)[:, :, None]
    if direct:
        full = solve(
            obs_count, coef_count, observations, design, shifts[:, None], keep, gain
        )
    else:
        full = solve_plain(coef_count, observations, design, shifts[:, None], keep, gain)
    block_count = coef_count * BPO
    block_rows = NL // block_count
    owned_rows = kdev // NL
    block_ids = jnp.arange(block_count, dtype=jnp.int32)
    position = jnp.sum(
        jnp.where(order_map[:, None] == block_ids[None, :], block_ids[:, None], 0), axis=0
    )
    paired_row = coef_perm // NL
    column = coef_perm % NL
    place_of = jnp.sum(
        jnp.where(
            (paired_row // block_rows)[None, :] == block_ids[:, None], position[:, None], 0
        ),
        axis=0,
    )
    owner_row = place_of * block_rows + paired_row % block_rows
    lanes = owned_rows * COLS
    if direct and owned_rows % (2 * obs_count) == 0:
        local = share(obs_count, coef_count, owner_row[None, :], column[None, :], full)
    else:
        placed = place(owner_row[None, :], column[None, :], full)
        outgoing = placed.astype(jnp.bfloat16).reshape(coef_count, lanes, NL)
        local = coef_scatter(outgoing, coef_count, 5)
    my_blocks = lax.dynamic_slice_in_dim(order_map, coef_rank * BPO, BPO)
    row_offsets = jnp.arange(block_rows, dtype=jnp.int32)
    owned_canon = (my_blocks[:, None] * block_rows + row_offsets[None, :]).reshape(owned_rows)
    lat_block = LAT_DEV * coef_count
    lat_total = lat_block * obs_count
    lat_ids = obs_rank * lat_block + jnp.arange(lat_block, dtype=jnp.int32)
    colatitude = math.pi * (lat_ids.astype(jnp.float32) + 0.5) / lat_total
    orders = jnp.repeat(owned_canon, COLS).astype(jnp.float32)
    parts = legendre(orders, colatitude, local).reshape(2, lat_block, owned_rows, COLS)
    band = parts.transpose(2, 0, 3, 1)
    own_cos, own_sin = wave_tables(owned_canon, NLON)
    first_sum = jnp.einsum("lqc,qk->lck", parts[0], own_cos, precision=lax.Precision.HIGHEST)
    second_sum = jnp.einsum("lqc,qk->lck", parts[1], own_sin, precision=lax.Precision.HIGHEST)
    shares = ((first_sum + second_sum) / math.sqrt(NL)).reshape(
        coef_count, LAT_DEV * COLS, NLON
    )
    field = coef_scatter(shares, coef_count, 6).reshape(LAT_DEV, COLS, NLON).transpose(1, 0, 2)
    return (band, field)


def solution(mesh):
    placed = (P("obs", "coef"), P(None, "obs"), P(), P(), P("coef"), P())
    return jax.shard_map(
        body,
        mesh=mesh,
        in_specs=placed,
        out_specs=(P("coef", None, None, "obs"), P(None, ("obs", "coef"), None)),
        check_vma=False,
    )
```
